256 devices in a mesh: coil: 32 (over z, y), slab: 8 (over x, core).
Axes of the slice: x: 4, y: 4, z: 8, core: 2. Of those that a mesh axis runs over, the one named last changes fastest.
Arguments:
- cotangent: float32 [32, 2, 256, 256], P('coil', None, 'slab'), may hold values from -60 to 60
- saved_solution: float32 [32, 2, 256, 256], P('coil', None, 'slab'), may hold values from -6 to 6
- coil_maps: bfloat16 [32, 32, 2, 256, 256], P('coil', None, None, 'slab'), may hold values from -1.5 to 1.5
- kspace: bfloat16 [32, 32, 2, 256, 256], P('coil', None, None, 'slab'), may hold values from -6 to 6
- mask_logit: float32 [32, 256], P(None, 'slab'), may hold values from -4.5 to 4.5
- reach: int32 [32, 256], P(None, 'slab'), may hold values from 0 to 256, as said below
Outputs:
- image_grad: float32 [32, 2, 256, 256], P('coil', None, 'slab')
- kspace_grad: bfloat16 [32, 32, 2, 256, 256], P('coil', None, None, 'slab')
- logit_grad: float32 [32, 256], P(None, 'slab')
The draws below stay inside these ranges and needn't reach their ends.
Inputs may be any that keep to these rules, and one draw needn't show every extreme that they name: reach[z, y] is 0 (line not acquired) or between 128 and 256; line [0, 0] is always fully acquired and line [0, 128] never.
All inputs are finite; a program needn't handle non-finite values.
Results may differ from the reference program's by a relative error of at most 0.02.
Values may be sent and summed in bfloat16 or wider, within the bound.
A program may use at most 64 MiB of HBM per device.

```python
import math
import jax
import jax.numpy as jnp
from jax import lax

NX = 256
NY = 256
NZ = 32
ITERS = 2
COILS = 32


def draw_cotangent(key, part):
    base_key, column_key = jax.random.split(jax.random.fold_in(key, 11))
    shape = (NZ, 2, NX, NY)
    base = jnp.clip(jax.random.normal(base_key, shape, jnp.float32), -5.0, 5.0)
    rise = 3.0
    slice_pos = jnp.arange(NZ, dtype=jnp.float32) / max(NZ - 1, 1)
    readout_pos = jnp.arange(NX, dtype=jnp.float32) / max(NX - 1, 1)
    ramp = rise ** (slice_pos[:, None, None, None] + readout_pos[None, None, :, None] - 1.0)
    column = jnp.exp(jax.random.uniform(column_key, (NY,), jnp.float32, -0.5 * math.log(10.0), 0.5 * math.log(10.0)))
    return base * ramp * column[None, None, None, :]


def draw_reach(key, part):
    pick_key, extent_key = jax.random.split(jax.random.fold_in(key, 23))
    acquired = jax.random.randint(pick_key, (NZ, NY), 0, 5) >= 2
    extent = jax.random.randint(extent_key, (NZ, NY), NX // 2, NX + 1)
    values = jnp.where(acquired, extent, 0).astype(jnp.int32)
    values = values.at[0, 0].set(NX)
    values = values.at[0, NY // 2].set(0)
    return values


def with_spikes(values, key, source, target, shards_of, factor):
    def block_of(axis_at):
        return (jnp.arange(values.shape[axis_at]) // (values.shape[axis_at] // shards_of)).reshape((-1,) + (1,) * (values.ndim - 1 - axis_at))

    one_side = jax.random.permutation(key, shards_of)[block_of(target)]
    other_side = (block_of(target) + shards_of // 2) % shards_of
    return jnp.where((block_of(source) == one_side) | (block_of(source) == other_side), factor * values, values)


def block_levels(rng, shape, cuts, low, high):
    gain = 1.0
    for dim, blocks in cuts:
        steps = jax.random.uniform(jax.random.fold_in(jax.random.fold_in(rng, 6), dim), (blocks,), jnp.float32, low / len(cuts), high / len(cuts))
        gain = gain * jnp.repeat(jnp.exp(steps), shape[dim] // blocks).reshape((-1,) + (1,) * (len(shape) - 1 - dim))
    return gain


def normal_values(stream_key, shape, deviation, bound, pieces=(), kind=jnp.bfloat16):
    array = jax.random.normal(stream_key, shape, jnp.float32) * deviation
    if len(pieces) > 0:
        array = block_levels(stream_key, shape, pieces, -0.22, 0.18) * array
    return jnp.clip(array, min=-bound, max=bound).astype(kind)


def gaussian_with(rng, dims, deviation, most, cuts, heavy, held_as=jnp.bfloat16):
    result = deviation * jax.random.normal(rng, dims, jnp.float32)
    if cuts:
        result = result * block_levels(rng, dims, cuts, -0.22, 0.18)
    return jnp.clip(with_spikes(result, jax.random.fold_in(rng, 3), *heavy), -most, most).astype(held_as)


def setup_inputs(seed: int = 0) -> dict:
    splits = jax.random.split(jax.random.key(seed), 7)
    cotangent = draw_cotangent(jax.random.fold_in(splits[6], 71), 0)
    saved_solution = normal_values(splits[1], (NZ, 2, NX, NY), 1.0, 6.0, ((0, 32), (2, 8)), jnp.float32)
    coil_maps = gaussian_with(splits[2], (COILS, NZ, 2, NX, NY), (1.0 / (2 * COILS) ** 0.5), 1.5, ((0, 32), (3, 8)), (0, 1, 32, 2.75))
    kspace = normal_values(splits[3], (COILS, NZ, 2, NY, NX), 1.0, 6.0, ((0, 32), (3, 8)))
    mask_logit = normal_values(splits[4], (NZ, NY), 1.5, 4.5, ((1, 8),), jnp.float32)
    reach = draw_reach(jax.random.fold_in(splits[6], 71), 0)
    return {"cotangent": cotangent, "saved_solution": saved_solution, "coil_maps": coil_maps, "kspace": kspace, "mask_logit": mask_logit, "reach": reach}


DAMPING = 0.2

def dft_table(length, sign):
    index = jnp.arange(length, dtype=jnp.int32)
    phase = (index[:, None] * index[None, :] % length).astype(jnp.float32) * (2.0 * math.pi / length)
    factor = 1.0 / math.sqrt(length)
    cosine = jnp.cos(phase) * factor
    sine = sign * jnp.sin(phase) * factor
    table = jnp.stack([jnp.stack([cosine, sine], axis=1), jnp.stack([-sine, cosine], axis=1)], axis=0)
    return table.astype(jnp.bfloat16)

def complex_product(factor, operand):
    factor_re, factor_im = (factor[:, 0], factor[:, 1])
    operand_re, operand_im = (operand[:, 0], operand[:, 1])
    return jnp.stack([factor_re * operand_re - factor_im * operand_im, factor_re * operand_im + factor_im * operand_re], axis=1)

def conjugate_product(factor, operand):
    factor_re, factor_im = (factor[:, 0], factor[:, 1])
    operand_re, operand_im = (operand[:, 0], operand[:, 1])
    return jnp.stack([factor_re * operand_re + factor_im * operand_im, factor_re * operand_im - factor_im * operand_re], axis=1)

def mixing(form, values, table):
    return jnp.einsum(form, values.astype(jnp.float32), table.astype(jnp.float32))

def reference(cotangent, saved_solution, coil_maps, kspace, mask_logit, reach):
    y_fwd, y_inv = (dft_table(NY, -1.0), dft_table(NY, 1.0))
    z_fwd, z_inv = (dft_table(NZ, -1.0), dft_table(NZ, 1.0))
    x_fwd, x_inv = (dft_table(NX, -1.0), dft_table(NX, 1.0))
    readout = jnp.arange(NX, dtype=jnp.int32)
    centred = (readout + NX // 2) % NX
    sampled = (centred[None, None, :] >= (NX - reach)[:, :, None]).astype(jnp.float32)
    gate = jax.nn.sigmoid(mask_logit)
    weight = sampled * gate[:, :, None]
    squared = (weight * weight)[:, None]

    def forward(maps, image_bf):
        product = complex_product(maps.astype(jnp.float32), image_bf.astype(jnp.float32)).astype(jnp.bfloat16)
        rows = mixing('zixn,inok->zoxk', product, y_fwd).astype(jnp.bfloat16)
        mixed = mixing('nixk,inom->moxk', rows, z_fwd).astype(jnp.bfloat16)
        return mixing('zink,inoq->zokq', mixed, x_fwd)

    def backward(maps, spectrum):
        mixed = mixing('zikq,iqon->zonk', spectrum, x_inv).astype(jnp.bfloat16)
        rows = mixing('mixk,imon->noxk', mixed, z_inv).astype(jnp.bfloat16)
        image = mixing('zixk,ikon->zoxn', rows, y_inv)
        return conjugate_product(maps.astype(jnp.float32), image)

    def operator(direction):
        image_bf = direction.astype(jnp.bfloat16)

        def add_coil(total, maps):
            spectrum = (squared * forward(maps, image_bf)).astype(jnp.bfloat16)
            term = lax.optimization_barrier(backward(maps, spectrum).astype(jnp.bfloat16))
            return (total + term.astype(jnp.float32), None)
        total, unused = lax.scan(add_coil, jnp.zeros(direction.shape, jnp.float32), coil_maps)
        return total + DAMPING * direction
    residual = cotangent
    direction = cotangent
    solution = jnp.zeros(cotangent.shape, jnp.float32)
    norm_now = jnp.sum(residual * residual)
    for step in range(ITERS):
        image = operator(direction)
        alpha = norm_now / jnp.sum(direction * image)
        solution = solution + alpha * direction
        if step + 1 < ITERS:
            residual = residual - alpha * image
            norm_next = jnp.sum(residual * residual)
            direction = residual + norm_next / norm_now * direction
            norm_now = norm_next
    image_grad = DAMPING * solution
    solution_bf = solution.astype(jnp.bfloat16)
    saved_bf = saved_solution.astype(jnp.bfloat16)
    weight_wide = weight[:, None]

    def per_coil(total, inputs):
        maps, data = inputs
        spectrum = forward(maps, solution_bf)
        saved_k = forward(maps, saved_bf)
        grad = (weight_wide * spectrum).astype(jnp.bfloat16)
        data_f = data.astype(jnp.float32)
        value = spectrum[:, 0] * (data_f[:, 0] - 2.0 * weight * saved_k[:, 0]) + spectrum[:, 1] * (data_f[:, 1] - 2.0 * weight * saved_k[:, 1])
        return (total + gate * (1.0 - gate) * lax.optimization_barrier(jnp.sum(sampled * value, axis=2)), grad)
    logit_grad, kspace_grad = lax.scan(per_coil, jnp.zeros((NZ, NY), jnp.float32), (coil_maps, kspace))
    return (image_grad, kspace_grad, logit_grad)
```

```python
import math

import jax
import jax.numpy as jnp
from jax import lax
from jax.sharding import PartitionSpec as P

NX = 256
NY = 256
NZ = 32
ITERS = 2


DAMPING = 0.2


def dft_table(length, sign):
    index = jnp.arange(length, dtype=jnp.int32)
    phase = (index[:, None] * index[None, :] % length).astype(jnp.float32) * (
        2.0 * math.pi / length
    )
    factor = 1.0 / math.sqrt(length)
    cosine = jnp.cos(phase) * factor
    sine = sign * jnp.sin(phase) * factor
    table = jnp.stack(
        [jnp.stack([cosine, sine], axis=1), jnp.stack([-sine, cosine], axis=1)], axis=0
    )
    return table.astype(jnp.bfloat16)


def complex_product(factor, operand):
    factor_re, factor_im = (factor[:, 0], factor[:, 1])
    operand_re, operand_im = (operand[:, 0], operand[:, 1])
    return jnp.stack(
        [
            factor_re * operand_re - factor_im * operand_im,
            factor_re * operand_im + factor_im * operand_re,
        ],
        axis=1,
    )


def conjugate_product(factor, operand):
    factor_re, factor_im = (factor[:, 0], factor[:, 1])
    operand_re, operand_im = (operand[:, 0], operand[:, 1])
    return jnp.stack(
        [
            factor_re * operand_re + factor_im * operand_im,
            factor_re * operand_im - factor_im * operand_re,
        ],
        axis=1,
    )


def shards(cotangent, saved_solution, coil_maps, kspace, mask_logit, reach):
    y_fwd, y_inv = (dft_table(NY, -1.0), dft_table(NY, 1.0))
    z_fwd, z_inv = (dft_table(NZ, -1.0), dft_table(NZ, 1.0))
    x_fwd, x_inv = (dft_table(NX, -1.0), dft_table(NX, 1.0))
    maps = coil_maps[0]
    data = kspace[0].astype(jnp.float32)
    readout = jnp.arange(NX, dtype=jnp.int32)
    centred = (readout + NX // 2) % NX
    sampled = (centred[None, None, :] >= (NX - reach)[:, :, None]).astype(jnp.float32)
    gate = jax.nn.sigmoid(mask_logit)
    weight = sampled * gate[:, :, None]
    squared = (weight * weight)[:, None]

    def front(piece):
        product = complex_product(maps.astype(jnp.float32), piece.astype(jnp.float32)).astype(
            jnp.bfloat16
        )
        return jnp.einsum(
            "zixn,inok->zoxk", product, y_fwd, preferred_element_type=jnp.float32
        ).astype(jnp.bfloat16)

    def gathered_front(shard):
        return front(lax.all_gather(shard, "coil", axis=0, tiled=True))

    def to_kspace(rows):
        mixed = jnp.einsum(
            "nixk,inom->moxk", rows, z_fwd, preferred_element_type=jnp.float32
        ).astype(jnp.bfloat16)
        swapped = lax.all_to_all(mixed, "slab", split_axis=3, concat_axis=2, tiled=True)
        return jnp.einsum("zink,inoq->zokq", swapped, x_fwd, preferred_element_type=jnp.float32)

    direction = cotangent
    both = ("coil", "slab")
    saved_k = to_kspace(gathered_front(saved_solution.astype(jnp.bfloat16)))
    first_k = to_kspace(gathered_front(direction.astype(jnp.bfloat16)))
    first_w = weight[:, None] * first_k
    norm_now, first_energy = lax.psum(
        (jnp.sum(direction * direction), jnp.sum(first_w * first_w)), both
    )
    apply_spectrum = (squared * first_k).astype(jnp.bfloat16)
    to_mixed = jnp.einsum(
        "zikq,iqon->zonk", apply_spectrum, x_inv, preferred_element_type=jnp.float32
    ).astype(jnp.bfloat16)
    to_swapped = lax.all_to_all(to_mixed, "slab", split_axis=2, concat_axis=3, tiled=True)
    apply_image_rows = jnp.einsum(
        "mixk,imon->noxk", to_swapped, z_inv, preferred_element_type=jnp.float32
    ).astype(jnp.bfloat16)
    image = jnp.einsum(
        "zixk,ikon->zoxn", apply_image_rows, y_inv, preferred_element_type=jnp.float32
    )
    summed = lax.psum_scatter(
        conjugate_product(maps.astype(jnp.float32), image).astype(jnp.bfloat16),
        "coil",
        scatter_dimension=0,
        tiled=True,
    ).astype(jnp.float32)
    image = summed + DAMPING * direction
    alpha = norm_now / (first_energy + DAMPING * norm_now)
    residual = direction - alpha * image
    second_k = to_kspace(gathered_front(residual.astype(jnp.bfloat16)))
    second_w = weight[:, None] * second_k
    gain = gate * (1.0 - gate)
    target = data - 2.0 * weight[:, None] * saved_k

    def line_terms(spectrum):
        return gain * jnp.sum(sampled * jnp.sum(spectrum * target, axis=1), axis=2)

    norm_next, crossing, second_energy, mixed_energy = lax.psum(
        (
            jnp.sum(residual * residual),
            jnp.sum(residual * direction),
            jnp.sum(second_w * second_w),
            jnp.sum(second_w * first_w),
        ),
        both,
    )
    lines = lax.psum(jnp.stack([line_terms(first_k), line_terms(second_k)]), "coil")
    beta = norm_next / norm_now
    curvature = (second_energy + beta * (2.0 * mixed_energy + beta * first_energy)) + DAMPING * (
        norm_next + beta * (2.0 * crossing + beta * norm_now)
    )
    later = norm_next / curvature
    early = alpha + later * beta
    image_grad = DAMPING * (early * direction + later * residual)
    kspace_grad = (early * first_w + later * second_w).astype(jnp.bfloat16)[None]
    logit_grad = early * lines[0] + later * lines[1]
    return (image_grad, kspace_grad, logit_grad)


def solution(mesh):
    placed = (
        P("coil", None, "slab", None),
        P("coil", None, "slab", None),
        P("coil", None, None, "slab", None),
        P("coil", None, None, "slab", None),
        P(None, "slab"),
        P(None, "slab"),
    )
    return jax.shard_map(
        shards,
        mesh=mesh,
        in_specs=placed,
        out_specs=(
            P("coil", None, "slab", None),
            P("coil", None, None, "slab", None),
            P(None, "slab"),
        ),
        check_vma=False,
    )
```

```python
import jax
import jax.numpy as jnp
import numpy as np
from jax import lax
from jax.experimental import pallas as pl
from jax.experimental.pallas import tpu as pltpu
from jax.sharding import PartitionSpec as P

N = 256
NZ = 32
DAMPING = 0.2
DEPTH = 8
BREADTH = 4
NEAREST = (1, 7, 2, 6, 3, 5, 4)
MESH = pl.DeviceIdType.MESH
BF16 = jnp.bfloat16
F32 = jnp.float32


def tables():
    def cosine_sine(length):
        index = np.arange(length)
        phase = (index[:, None] * index[None, :] % length).astype(np.float32) * np.float32(
            2.0 * np.pi / length
        )
        factor = np.float32(1.0 / np.sqrt(length))
        return np.cos(phase) * factor, np.sin(phase) * factor

    plane = np.stack(cosine_sine(N))
    eye = np.eye(8, dtype=np.float32)
    depth = np.stack([np.kron(part, eye) for part in cosine_sine(NZ)])
    return jnp.asarray(plane, BF16), jnp.asarray(depth, BF16)


def dot(left, right, dims=((1,), (0,))):
    return lax.dot_general(left, right, (dims, ((), ())), preferred_element_type=F32)


def call(body, out_shape, scratch=(), collective=None, name=None):
    params = dict(vmem_limit_bytes=60 * 1024 * 1024)
    if collective is not None:
        params.update(collective_id=collective, has_side_effects=True)
    many = isinstance(out_shape, (tuple, list))

    def run(*args):
        return pl.pallas_call(
            body,
            out_shape=out_shape,
            in_specs=[pl.BlockSpec(memory_space=pltpu.VMEM)] * len(args),
            out_specs=[pl.BlockSpec(memory_space=pltpu.VMEM)] * len(out_shape)
            if many
            else pl.BlockSpec(memory_space=pltpu.VMEM),
            scratch_shapes=list(scratch),
            compiler_params=pltpu.CompilerParams(**params),
            name=name,
        )(*args)

    return run


class Place:
    def __init__(self):
        self.coil = lax.axis_index("coil")
        self.slab = lax.axis_index("slab")
        self.z, self.y = self.coil // BREADTH, self.coil % BREADTH
        self.x, self.core = self.slab // 2, self.slab % 2

    def along_z(self, step):
        return ((self.z + step + DEPTH) % DEPTH) * BREADTH + self.y

    def along_y(self, step):
        return self.z * BREADTH + self.row(step)

    def row(self, step):
        return (self.y + step + BREADTH) % BREADTH

    def along_x(self, step, core):
        return ((self.x + step + 4) % 4) * 2 + core


def greet(place, planes, slabs, rows=False):
    barrier = pltpu.get_barrier_semaphore()
    targets = []
    if planes:
        targets += [(place.along_z(step), place.slab) for step in range(1, DEPTH)]
        targets += [(place.along_y(step), place.slab) for step in ((1, 2, 3) if rows else (1, 3))]
    if slabs:
        targets += [(place.coil, place.along_x(step, core)) for step in (1, 3) for core in (0, 1)]
        targets += [(place.coil, place.along_x(0, 1 - place.core))]
        if slabs > 1:
            targets += [(place.coil, place.along_x(2, core)) for core in (0, 1)]
    for target in targets:
        pl.semaphore_signal(barrier, inc=1, device_id=target, device_id_type=MESH)
    pl.semaphore_wait(barrier, len(targets))


def sender(sends, receives):
    started = []

    def start(source, target, number, arrival, device):
        copy = pltpu.make_async_remote_copy(
            src_ref=source,
            dst_ref=target,
            send_sem=sends.at[number],
            recv_sem=receives.at[arrival],
            device_id=device,
            device_id_type=MESH,
        )
        copy.start()
        started.append(copy)

    def arrived(target, arrival, device):
        pltpu.make_async_remote_copy(
            src_ref=target,
            dst_ref=target,
            send_sem=sends.at[0],
            recv_sem=receives.at[arrival],
            device_id=device,
            device_id_type=MESH,
        ).wait_recv()

    def drain():
        for copy in started:
            copy.wait_send()

    return start, arrived, drain


class Exchange:
    COPIES = 13

    def __init__(self, place, source, target, relay, sends, receives):
        self.p, self.source, self.target, self.relay = place, source, target, relay
        self.start, self.arrived, self.drain = sender(sends, receives)

    @staticmethod
    def scratch():
        return [
            pltpu.VMEM((2, 2, 2, 2, 32, N), BF16),
            pltpu.SemaphoreType.DMA((Exchange.COPIES,)),
            pltpu.SemaphoreType.DMA((Exchange.COPIES,)),
        ]

    def begin(self):
        p = self.p
        for way, step in ((0, 1), (1, -1)):
            for core in (0, 1):
                self.start(
                    self.source.at[p.along_x(2, core), pl.ds(2 * way, 2)],
                    self.relay.at[way, core],
                    way * 2 + core,
                    way * 2 + core,
                    (p.coil, p.along_x(step, p.core)),
                )
        for way, step in ((0, 1), (1, -1)):
            for core in (0, 1):
                self.start(
                    self.source.at[p.along_x(step, core)],
                    self.target.at[p.slab],
                    4 + way * 2 + core,
                    4 + way * 2 + p.core,
                    (p.coil, p.along_x(step, core)),
                )
        partner = p.along_x(0, 1 - p.core)
        self.start(self.source.at[partner], self.target.at[p.slab], 12, 12, (p.coil, partner))
        self.target[p.slab] = self.source[p.slab]

    def forward(self):
        p = self.p
        for way, step in ((0, 1), (1, -1)):
            for core in (0, 1):
                self.arrived(
                    self.relay.at[way, core], way * 2 + core, (p.coil, p.along_x(-step, p.core))
                )
                self.start(
                    self.relay.at[way, core],
                    self.target.at[p.along_x(-step, p.core), pl.ds(2 * way, 2)],
                    8 + way * 2 + core,
                    8 + way * 2 + p.core,
                    (p.coil, p.along_x(step, core)),
                )

    def finish(self):
        p = self.p
        partner = p.along_x(0, 1 - p.core)
        self.arrived(self.target.at[partner], 12, (p.coil, partner))
        for way, step in ((0, 1), (1, -1)):
            for core in (0, 1):
                near = p.along_x(-step, core)
                self.arrived(self.target.at[near], 4 + way * 2 + core, (p.coil, near))
        for way, step in ((0, 1), (1, -1)):
            for core in (0, 1):
                far = p.along_x(2, core)
                self.arrived(
                    self.target.at[far, pl.ds(2 * way, 2)], 8 + way * 2 + core, (p.coil, far)
                )
        self.drain()


class Gather:
    COPIES = 39

    def __init__(self, place, source, target, sends, receives):
        self.p, self.source, self.target = place, source, target
        self.start, self.arrived, self.drain = sender(sends, receives)

    @staticmethod
    def scratch():
        return [
            pltpu.SemaphoreType.DMA((Gather.COPIES,)),
            pltpu.SemaphoreType.DMA((Gather.COPIES,)),
        ]

    def slice_of(self, order, row_step):
        p = self.p
        back = 0 if order == 0 else NEAREST[order - 1]
        return ((p.z - back + DEPTH) % DEPTH) * BREADTH + p.row(row_step)

    def pass_on(self, order, source):
        p = self.p
        slot = self.slice_of(order, 0)
        for way, step in ((0, 1), (1, -1)):
            number = 7 + order * 2 + way
            self.start(source, self.target.at[slot], number, number, (p.along_y(step), p.slab))

    def begin(self):
        p = self.p
        for order, step in enumerate(NEAREST):
            self.start(
                self.source, self.target.at[p.coil], order, order, (p.along_z(step), p.slab)
            )
        self.pass_on(0, self.source)
        self.target[p.coil] = self.source[...]

    def spread(self):
        p = self.p
        for order, step in enumerate(NEAREST):
            slot = self.slice_of(order + 1, 0)
            self.arrived(self.target.at[slot], order, (p.along_z(-step), p.slab))
            self.pass_on(order + 1, self.target.at[slot])

    def forward(self):
        p = self.p
        for order in range(DEPTH):
            for way, step in ((0, 1), (1, -1)):
                slot = self.slice_of(order, -step)
                self.arrived(
                    self.target.at[slot], 7 + order * 2 + way, (p.along_y(-step), p.slab)
                )
                number = 23 + order * 2 + way
                half = self.target.at[slot, pl.ds(way, 1)]
                self.start(half, half, number, number, (p.along_y(step), p.slab))

    def finish(self):
        p = self.p
        for order in range(DEPTH):
            for way, step in ((0, 1), (1, -1)):
                slot = self.slice_of(order, 2)
                self.arrived(
                    self.target.at[slot, pl.ds(way, 1)],
                    23 + order * 2 + way,
                    (p.along_y(-step), p.slab),
                )
        self.drain()


class Scatter:
    COPIES = 13

    def __init__(self, place, terms, far, near, mixed, rows, column, sends, receives):
        self.p, self.terms = place, terms
        self.far, self.near, self.mixed, self.rows, self.column = far, near, mixed, rows, column
        self.start, self.arrived, self.drain = sender(sends, receives)

    @staticmethod
    def scratch():
        return [
            pltpu.VMEM((2, DEPTH, 32, N), BF16),
            pltpu.VMEM((2, 2, DEPTH, 32, N), BF16),
            pltpu.VMEM((2, DEPTH, 32, N), BF16),
            pltpu.VMEM((DEPTH, 2, 32, N), BF16),
            pltpu.VMEM((DEPTH - 1, 2, 32, N), BF16),
            pltpu.SemaphoreType.DMA((Scatter.COPIES,)),
            pltpu.SemaphoreType.DMA((Scatter.COPIES,)),
        ]

    def begin(self):
        p = self.p
        for way, step in ((0, 1), (1, -1)):
            beside = (p.along_y(step), p.slab)
            self.start(self.terms.at[:, p.row(2), way], self.far.at[way], way, way, beside)
        for way, step in ((0, 1), (1, -1)):
            beside = (p.along_y(step), p.slab)
            self.start(
                self.terms.at[:, p.row(step), 1 - way],
                self.near.at[way, 1 - way],
                2 + way,
                2 + way,
                beside,
            )

    def forward(self):
        p = self.p
        for way, step in ((0, 1), (1, -1)):
            beside = (p.along_y(step), p.slab)
            self.arrived(self.far.at[way], way, (p.along_y(-step), p.slab))
            self.mixed[way] = (
                self.far[way].astype(F32) + self.terms[:, p.row(step), way].astype(F32)
            ).astype(BF16)
            self.start(self.mixed.at[way], self.near.at[way, way], 4 + way, 4 + way, beside)

    def columns(self):
        p = self.p
        for way, step in ((0, 1), (1, -1)):
            beside = (p.along_y(-step), p.slab)
            self.arrived(self.near.at[way, 1 - way], 2 + way, beside)
            self.arrived(self.near.at[way, way], 4 + way, beside)
        for part in (0, 1):
            self.rows[:, part] = (
                self.terms[:, p.row(0), part].astype(F32)
                + self.near[0, part].astype(F32)
                + self.near[1, part].astype(F32)
            ).astype(BF16)
        for order, step in enumerate(NEAREST):
            self.start(
                self.rows.at[(p.z + step) % DEPTH],
                self.column.at[order],
                6 + order,
                6 + order,
                (p.along_z(step), p.slab),
            )

    def total(self):
        p = self.p
        value = self.rows[p.z].astype(F32)
        for order, step in enumerate(NEAREST):
            self.arrived(self.column.at[order], 6 + order, (p.along_z(-step), p.slab))
            value = value + self.column[order].astype(F32)
        return value


class Total:
    COPIES = 17

    def __init__(self, place, held, shared, sends, receives):
        self.p, self.held, self.shared = place, held, shared
        self.start, self.arrived, self.drain = sender(sends, receives)

    @staticmethod
    def scratch(height, shared):
        return [
            pltpu.VMEM((12, height, 128), F32),
            pltpu.VMEM((8, shared, 128), F32),
            pltpu.SemaphoreType.DMA((Total.COPIES,)),
            pltpu.SemaphoreType.DMA((Total.COPIES,)),
        ]

    def along_z(self, value):
        p = self.p
        self.held[p.z] = value
        for order, step in enumerate(NEAREST):
            self.start(
                self.held.at[p.z], self.held.at[p.z], order, order, (p.along_z(step), p.slab)
            )

    def sum_z(self):
        p = self.p
        for order, step in enumerate(NEAREST):
            self.arrived(
                self.held.at[(p.z - step + DEPTH) % DEPTH], order, (p.along_z(-step), p.slab)
            )
        value = self.held[0]
        for place in range(1, DEPTH):
            value = value + self.held[place]
        return value

    def along_y(self, value):
        p = self.p
        self.held[DEPTH + p.y] = value
        for step in (1, 2, 3):
            self.start(
                self.held.at[DEPTH + p.y],
                self.held.at[DEPTH + p.y],
                6 + step,
                6 + step,
                (p.along_y(step), p.slab),
            )

    def sum_y(self):
        p = self.p
        for step in (1, 2, 3):
            self.arrived(
                self.held.at[DEPTH + p.row(-step)], 6 + step, (p.along_y(-step), p.slab)
            )
        value = self.held[DEPTH]
        for place in range(1, BREADTH):
            value = value + self.held[DEPTH + place]
        return value

    def along_slab(self, value):
        p = self.p
        self.shared[p.slab] = value
        for step in range(1, 8):
            self.start(
                self.shared.at[p.slab],
                self.shared.at[p.slab],
                9 + step,
                9 + step,
                (p.coil, (p.slab + step) % 8),
            )

    def sum_slab(self):
        p = self.p
        for step in range(1, 8):
            back = (p.slab - step + 8) % 8
            self.arrived(self.shared.at[back], 9 + step, (p.coil, back))
        value = self.shared[0]
        for place in range(1, 8):
            value = value + self.shared[place]
        return value


def gather_kernel(source, target, *scratch):
    place = Place()
    greet(place, True, 0)
    gather = Gather(place, source, target, *scratch)
    gather.begin()
    gather.spread()
    gather.forward()
    gather.finish()


def exchange_kernel(source, target, *scratch):
    place = Place()
    greet(place, False, 1)
    exchange = Exchange(place, source, target, *scratch)
    exchange.begin()
    exchange.forward()
    exchange.finish()


def back_kernel(blocks, saved, sums, blocks_out, saved_out, sums_out, *scratch):
    place = Place()
    greet(place, True, 2, rows=True)
    exchange = Exchange(place, blocks, blocks_out, *scratch[:3])
    gather = Gather(place, saved, saved_out, *scratch[3:5])
    total = Total(place, *scratch[5:])
    total.along_z(sums[...])
    exchange.begin()
    gather.begin()
    total.along_y(total.sum_z())
    gather.spread()
    exchange.forward()
    total.along_slab(total.sum_y())
    gather.forward()
    sums_out[...] = total.sum_slab()
    exchange.finish()
    gather.finish()
    total.drain()


def whole(value):
    return jnp.sum(jnp.sum(value, axis=1, keepdims=True), axis=0, keepdims=True)


def turn_kernel(
    terms, blocks, direction, sums, blocks_out, residual_out, gathered, held, *scratch
):
    place = Place()
    greet(place, True, 1)
    scatter = Scatter(place, terms, *scratch[:7])
    exchange = Exchange(place, blocks, blocks_out, *scratch[7:10])
    gather = Gather(place, held, gathered, *scratch[10:12])
    scatter.begin()
    exchange.begin()
    scatter.forward()
    exchange.forward()
    scatter.columns()
    norm, energy = whole(sums[0:8]), whole(sums[8:16])
    alpha = norm / (energy + DAMPING * norm)
    current = direction[...]
    image = scatter.total() + DAMPING * current
    residual = current - alpha[None] * image
    residual_out[...] = residual
    held[...] = residual.astype(BF16)
    gather.begin()
    gather.spread()
    gather.forward()
    exchange.finish()
    gather.finish()
    scatter.drain()


def total_kernel(values, values_out, *scratch):
    place = Place()
    greet(place, True, 2, rows=True)
    total = Total(place, *scratch)
    total.along_z(values[...])
    total.along_y(total.sum_z())
    value = total.sum_y()
    values_out[0:32] = value[0:32]
    total.along_slab(value[32:40])
    values_out[32:40] = total.sum_slab()
    total.drain()


def front(maps, image, plane, out):
    cosine, sine = plane[0], plane[1]

    def group(g, carry):
        part = pl.ds(g * 8, 8)
        maps_re, maps_im = maps[part, 0].astype(F32), maps[part, 1].astype(F32)
        image_re, image_im = image[part, 0].astype(F32), image[part, 1].astype(F32)
        real = (maps_re * image_re - maps_im * image_im).astype(BF16).reshape(N, N)
        imag = (maps_re * image_im + maps_im * image_re).astype(BF16).reshape(N, N)
        both = ((1,), (1,))
        rows_re = dot(cosine, real, both) + dot(sine, imag, both)
        rows_im = dot(cosine, imag, both) - dot(sine, real, both)
        out[:, g, 0] = rows_re.astype(BF16).reshape(8, 32, N)
        out[:, g, 1] = rows_im.astype(BF16).reshape(8, 32, N)
        return carry

    lax.fori_loop(0, 4, group, 0)


def spectrum(blocks, plane, wide):
    cosine, sine = plane[0], plane[1]

    def lines(g, part):
        pieces = [blocks[s, g, part] for s in range(8)]
        return jnp.concatenate(
            [
                jnp.concatenate([piece[:, 32 * k : 32 * k + 32] for piece in pieces], axis=1)
                for k in range(8)
            ],
            axis=0,
        )

    def group(g, carry):
        real, imag = lines(g, 0), lines(g, 1)
        wide[pl.ds(g * 8, 8), 0] = (dot(real, cosine) + dot(imag, sine)).reshape(8, 32, N)
        wide[pl.ds(g * 8, 8), 1] = (dot(imag, cosine) - dot(real, sine)).reshape(8, 32, N)
        return carry

    lax.fori_loop(0, 4, group, 0)


def strip(ref, part, at):
    return ref[:, part, at, :].reshape(N, N).astype(BF16)


def across(cosine, sine, real, imag):
    return (
        (dot(cosine, real) + dot(sine, imag)).reshape(NZ, 8, N),
        (dot(cosine, imag) - dot(sine, real)).reshape(NZ, 8, N),
    )


def fold(value):
    return jnp.sum(value[:, :, :128] + value[:, :, 128:], axis=0)


def apply_kernel(blocks, weight, plane, depth, kept, energy, out, wide):
    spectrum(blocks, plane, wide)
    cosine_z, sine_z = depth[0], depth[1]

    def chunk(c, total):
        at = pl.ds(pl.multiple_of(c * 8, 8), 8)
        real, imag = across(cosine_z, sine_z, strip(wide, 0, at), strip(wide, 1, at))
        kept[:, 0, at, :] = real
        kept[:, 1, at, :] = imag
        scale = weight[:, at, :]
        real, imag = scale * real, scale * imag
        total = total + fold(real * real + imag * imag)
        real = (scale * real).astype(BF16).reshape(N, N)
        imag = (scale * imag).astype(BF16).reshape(N, N)
        wide[:, 0, at, :] = (dot(cosine_z, real) - dot(sine_z, imag)).reshape(NZ, 8, N)
        wide[:, 1, at, :] = (dot(cosine_z, imag) + dot(sine_z, real)).reshape(NZ, 8, N)
        return total

    energy[...] = lax.fori_loop(0, 4, chunk, jnp.zeros((8, 128), F32))
    cosine, sine = plane[0], plane[1]

    def group(g, carry):
        part = pl.ds(g * 8, 8)
        real = wide[part, 0].reshape(N, N).astype(BF16)
        imag = wide[part, 1].reshape(N, N).astype(BF16)
        for which, value in (
            (0, dot(real, cosine) - dot(imag, sine)),
            (1, dot(imag, cosine) + dot(real, sine)),
        ):
            value = value.astype(BF16).reshape(8, 32, N)
            for s in range(8):
                out[s, g, which] = jnp.concatenate(
                    [value[k][:, 32 * s : 32 * s + 32] for k in range(8)], axis=1
                )
        return carry

    lax.fori_loop(0, 4, group, 0)


def image_kernel(blocks, maps, saved, plane, terms, saved_blocks):
    cosine, sine = plane[0], plane[1]

    def group(g, carry):
        real, imag = blocks[:, g, 0].reshape(N, N), blocks[:, g, 1].reshape(N, N)
        first = ((0,), (0,))
        image_re = (dot(real, cosine, first) - dot(imag, sine, first)).reshape(8, 32, N)
        image_im = (dot(imag, cosine, first) + dot(real, sine, first)).reshape(8, 32, N)
        part = pl.ds(g * 8, 8)
        maps_re, maps_im = maps[part, 0].astype(F32), maps[part, 1].astype(F32)
        terms[part, 0] = (maps_re * image_re + maps_im * image_im).astype(BF16)
        terms[part, 1] = (maps_re * image_im - maps_im * image_re).astype(BF16)
        return carry

    lax.fori_loop(0, 4, group, 0)
    front(maps, saved, plane, saved_blocks)


def front_kernel(maps, image, plane, out):
    front(maps, image, plane, out)


def close_kernel(
    blocks, saved_blocks, first, weight, data, residual, direction, plane, depth,
    kept, lines, wide, wide_saved,
):
    spectrum(blocks, plane, wide)
    spectrum(saved_blocks, plane, wide_saved)
    cosine_z, sine_z = depth[0], depth[1]
    residual_now, direction_now = residual[...], direction[...]

    def chunk(c, totals):
        at = pl.ds(pl.multiple_of(c * 8, 8), 8)
        real, imag = across(cosine_z, sine_z, strip(wide, 0, at), strip(wide, 1, at))
        kept[:, 0, at, :] = real
        kept[:, 1, at, :] = imag
        saved_re, saved_im = across(
            cosine_z, sine_z, strip(wide_saved, 0, at), strip(wide_saved, 1, at)
        )
        first_re, first_im = first[:, 0, at, :], first[:, 1, at, :]
        scale = weight[:, at, :]
        square = scale * scale
        second, mixed = totals
        second = second + fold(square * (real * real + imag * imag))
        mixed = mixed + fold(square * (real * first_re + imag * first_im))
        target_re = data[:, 0, at, :].astype(F32) - 2.0 * scale * saved_re
        target_im = data[:, 1, at, :].astype(F32) - 2.0 * scale * saved_im
        sampled = jnp.where(scale != 0.0, 1.0, 0.0)
        wide[:, 0, at, :] = sampled * (first_re * target_re + first_im * target_im)
        wide[:, 1, at, :] = sampled * (real * target_re + imag * target_im)
        return second, mixed

    zero = jnp.zeros((8, 128), F32)
    second, mixed = lax.fori_loop(0, 4, chunk, (zero, zero))
    lines[0:32, 0:32] = jnp.sum(wide[:, 0], axis=2)
    lines[0:32, 32:64] = jnp.sum(wide[:, 1], axis=2)
    lines[0:32, 64:128] = jnp.zeros((32, 64), F32)

    def narrow(value):
        value = value.reshape(64, N)
        return jnp.sum(value[:, :128] + value[:, 128:], axis=0, keepdims=True)

    lines[32:33] = jnp.sum(second, axis=0, keepdims=True)
    lines[33:34] = jnp.sum(mixed, axis=0, keepdims=True)
    lines[34:35] = narrow(residual_now * residual_now)
    lines[35:36] = narrow(residual_now * direction_now)
    lines[36:40] = jnp.zeros((4, 128), F32)


def shards(cotangent, saved_solution, coil_maps, kspace, mask_logit, reach):
    plane, depth = tables()
    maps = coil_maps[0]
    data = kspace[0]
    centred = (jnp.arange(N, dtype=jnp.int32) + N // 2) % N
    sampled = (centred[None, None, :] >= (N - reach)[:, :, None]).astype(F32)
    gate = jax.nn.sigmoid(mask_logit)
    weight = sampled * gate[:, :, None]
    direction = cotangent[0]
    blocks = jax.ShapeDtypeStruct((8, 4, 2, 32, N), BF16)
    image = jax.ShapeDtypeStruct((NZ, 2, 32, N), BF16)
    kept = jax.ShapeDtypeStruct((NZ, 2, 32, N), F32)
    wide = pltpu.VMEM((NZ, 2, 32, N), F32)
    square = jnp.sum((direction * direction).reshape(8, 16, 128), axis=1)

    gathered = call(gather_kernel, image, Gather.scratch(), 0, name="gather")(
        direction.astype(BF16)
    )
    sent = call(front_kernel, blocks, name="front")(maps, gathered, plane)
    rows = call(exchange_kernel, blocks, Exchange.scratch(), 1, name="exchange")(sent)
    first, energy, back = call(
        apply_kernel,
        (kept, jax.ShapeDtypeStruct((8, 128), F32), blocks),
        [wide],
        name="apply",
    )(rows, weight, plane, depth)
    sums = jnp.concatenate([square, energy], axis=0)
    returned, saved, sums = call(
        back_kernel,
        (blocks, image, jax.ShapeDtypeStruct((16, 128), F32)),
        Exchange.scratch() + Gather.scratch() + Total.scratch(16, 16),
        2,
        name="back",
    )(back, saved_solution[0].astype(BF16), sums)
    terms, saved_sent = call(image_kernel, (image, blocks), name="image")(
        returned, maps, saved, plane
    )
    slice_wide = jax.ShapeDtypeStruct((2, 32, N), F32)
    saved_rows, residual, gathered = call(
        turn_kernel,
        (blocks, slice_wide, image),
        [pltpu.VMEM((2, 32, N), BF16)]
        + Scatter.scratch()
        + Exchange.scratch()
        + Gather.scratch(),
        3,
        name="turn",
    )(terms.reshape(DEPTH, BREADTH, 2, 32, N), saved_sent, direction, sums)
    sent = call(front_kernel, blocks, name="front")(maps, gathered, plane)
    rows = call(exchange_kernel, blocks, Exchange.scratch(), 4, name="exchange2")(sent)
    second, lines = call(
        close_kernel,
        (kept, jax.ShapeDtypeStruct((40, 128), F32)),
        [wide, wide],
        name="close",
    )(rows, saved_rows, first, weight, data, residual, direction, plane, depth)
    lines = call(
        total_kernel,
        jax.ShapeDtypeStruct((40, 128), F32),
        Total.scratch(40, 8),
        5,
        name="total",
    )(lines)
    norm_now, first_energy = jnp.sum(sums[0:8]), jnp.sum(sums[8:16])
    alpha = norm_now / (first_energy + DAMPING * norm_now)
    scalars = jnp.sum(lines[32:36], axis=1)
    second_energy, mixed_energy, norm_next, crossing = [scalars[k] for k in range(4)]
    beta = norm_next / norm_now
    curvature = (second_energy + beta * (2.0 * mixed_energy + beta * first_energy)) + DAMPING * (
        norm_next + beta * (2.0 * crossing + beta * norm_now)
    )
    later = norm_next / curvature
    early = alpha + later * beta
    image_grad = (DAMPING * (early * direction + later * residual))[None]
    kspace_grad = (weight[:, None] * (early * first + later * second)).astype(BF16)[None]
    logit_grad = gate * (1.0 - gate) * (early * lines[0:32, 0:32] + later * lines[0:32, 32:64])
    return (image_grad, kspace_grad, logit_grad)


def solution(mesh):
    placed = (
        P("coil", None, "slab", None),
        P("coil", None, "slab", None),
        P("coil", None, None, "slab", None),
        P("coil", None, None, "slab", None),
        P(None, "slab"),
        P(None, "slab"),
    )
    return jax.shard_map(
        shards,
        mesh=mesh,
        in_specs=placed,
        out_specs=(
            P("coil", None, "slab", None),
            P("coil", None, None, "slab", None),
            P(None, "slab"),
        ),
        check_vma=False,
    )
```

```python
import jax
import jax.numpy as jnp
import numpy as np
from jax import lax
from jax.experimental import pallas as pl
from jax.experimental.pallas import tpu as pltpu
from jax.sharding import PartitionSpec as P

N = 256
NZ = 32
DAMPING = 0.2
DEPTH = 8
BREADTH = 4
NEAREST = (1, -1, 2, -2, 3, -3, 4)
PAIRS = ((0, 1), (-1, 2), (-2, 3), (-3, 4))
GROUPS = 4
MESH = pl.DeviceIdType.MESH
BF16 = jnp.bfloat16
F32 = jnp.float32


def tables():
    def cosine_sine(length):
        index = np.arange(length)
        phase = (index[:, None] * index[None, :] % length).astype(np.float32) * np.float32(
            2.0 * np.pi / length
        )
        factor = np.float32(1.0 / np.sqrt(length))
        return np.cos(phase) * factor, np.sin(phase) * factor

    plane = np.stack(cosine_sine(N))
    eye = np.eye(8, dtype=np.float32)
    depth = np.stack([np.kron(part, eye) for part in cosine_sine(NZ)])
    return jnp.asarray(plane, BF16), jnp.asarray(depth, BF16)


def dot(left, right, dims=((1,), (0,))):
    return lax.dot_general(left, right, (dims, ((), ())), preferred_element_type=F32)


class Place:
    def __init__(self):
        self.coil = lax.axis_index("coil")
        self.slab = lax.axis_index("slab")
        self.z, self.y = self.coil // BREADTH, self.coil % BREADTH
        self.x, self.core = self.slab // 2, self.slab % 2

    def first(self, step):
        return ((self.z + step + DEPTH) % DEPTH) * BREADTH

    def along_z(self, step):
        return self.first(step) + self.y

    def along_y(self, step):
        return self.z * BREADTH + self.row(step)

    def row(self, step):
        return (self.y + step + BREADTH) % BREADTH

    def along_x(self, step, core):
        return ((self.x + step + 4) % 4) * 2 + core


def greet(place):
    barrier = pltpu.get_barrier_semaphore()
    targets = [(place.along_z(step), place.slab) for step in range(1, DEPTH)]
    targets += [(place.along_y(step), place.slab) for step in range(1, BREADTH)]
    targets += [(place.coil, (place.slab + step) % 8) for step in range(1, 8)]
    for target in targets:
        pl.semaphore_signal(barrier, inc=1, device_id=target, device_id_type=MESH)
    pl.semaphore_wait(barrier, len(targets))


def sender(sends, receives):
    started = []

    def start(source, target, number, arrival, device):
        copy = pltpu.make_async_remote_copy(
            src_ref=source,
            dst_ref=target,
            send_sem=sends.at[number],
            recv_sem=receives.at[arrival],
            device_id=device,
            device_id_type=MESH,
        )
        copy.start()
        started.append(copy)

    def arrived(target, arrival, device):
        pltpu.make_async_remote_copy(
            src_ref=target,
            dst_ref=target,
            send_sem=sends.at[0],
            recv_sem=receives.at[arrival],
            device_id=device,
            device_id_type=MESH,
        ).wait_recv()

    def drain():
        for copy in started:
            copy.wait_send()

    return start, arrived, drain


class Exchange:
    COPIES = 13 * GROUPS

    def __init__(self, place, source, target, relay, sends, receives):
        self.p, self.source, self.target, self.relay = place, source, target, relay
        self.start, self.arrived, self.drain = sender(sends, receives)

    @staticmethod
    def scratch():
        return [
            pltpu.VMEM((GROUPS, 8, 2, 32, N), BF16),
            pltpu.VMEM((GROUPS, 8, 2, 32, N), BF16),
            pltpu.VMEM((GROUPS, 2, 2, 32, N), BF16),
            pltpu.SemaphoreType.DMA((Exchange.COPIES,)),
            pltpu.SemaphoreType.DMA((Exchange.COPIES,)),
        ]

    def begin(self, k):
        p, base = self.p, 13 * k
        for way, step in ((0, 1), (1, -1)):
            for core in (0, 1):
                self.start(
                    self.source.at[k, p.along_x(2, core), way],
                    self.relay.at[k, way, core],
                    base + way * 2 + core,
                    base + way * 2 + core,
                    (p.coil, p.along_x(step, p.core)),
                )
        for way, step in ((0, 1), (1, -1)):
            for core in (0, 1):
                self.start(
                    self.source.at[k, p.along_x(step, core)],
                    self.target.at[k, p.slab],
                    base + 4 + way * 2 + core,
                    base + 4 + way * 2 + p.core,
                    (p.coil, p.along_x(step, core)),
                )
        partner = p.along_x(0, 1 - p.core)
        self.start(
            self.source.at[k, partner],
            self.target.at[k, p.slab],
            base + 12,
            base + 12,
            (p.coil, partner),
        )
        self.target[k, p.slab] = self.source[k, p.slab]

    def forward(self, k):
        p, base = self.p, 13 * k
        for way, step in ((0, 1), (1, -1)):
            for core in (0, 1):
                self.arrived(
                    self.relay.at[k, way, core],
                    base + way * 2 + core,
                    (p.coil, p.along_x(-step, p.core)),
                )
                self.start(
                    self.relay.at[k, way, core],
                    self.target.at[k, p.along_x(-step, p.core), way],
                    base + 8 + way * 2 + core,
                    base + 8 + way * 2 + p.core,
                    (p.coil, p.along_x(step, core)),
                )

    def finish(self, k):
        p, base = self.p, 13 * k
        partner = p.along_x(0, 1 - p.core)
        self.arrived(self.target.at[k, partner], base + 12, (p.coil, partner))
        for way, step in ((0, 1), (1, -1)):
            for core in (0, 1):
                near = p.along_x(-step, core)
                self.arrived(self.target.at[k, near], base + 4 + way * 2 + core, (p.coil, near))
        for way, step in ((0, 1), (1, -1)):
            for core in (0, 1):
                far = p.along_x(2, core)
                self.arrived(
                    self.target.at[k, far, way], base + 8 + way * 2 + core, (p.coil, far)
                )


class Gather:
    COPIES = 39

    def __init__(self, place, source, target, sends, receives):
        self.p, self.source, self.target = place, source, target
        self.start, self.arrived, self.drain = sender(sends, receives)

    @staticmethod
    def scratch():
        return [
            pltpu.VMEM((2, 32, N), BF16),
            pltpu.VMEM((GROUPS, 2, BREADTH, 2, 32, N), BF16),
            pltpu.SemaphoreType.DMA((Gather.COPIES,)),
            pltpu.SemaphoreType.DMA((Gather.COPIES,)),
        ]

    @staticmethod
    def held(step):
        return next((k, pair.index(step)) for k, pair in enumerate(PAIRS) if step in pair)

    def pass_on(self, k, spot, source):
        p = self.p
        for way, step in ((0, 1), (1, -1)):
            number = 7 + (k * 2 + spot) * 2 + way
            self.start(
                source, self.target.at[k, spot, p.y], number, number, (p.along_y(step), p.slab)
            )

    def begin(self):
        p = self.p
        self.pass_on(0, 0, self.source)
        for order, step in enumerate(NEAREST):
            k, spot = self.held(step)
            self.start(
                self.source, self.target.at[k, spot, p.y], order, order, (p.along_z(-step), p.slab)
            )
        self.target[0, 0, p.y] = self.source[...]

    def spread(self, k):
        p = self.p
        for spot, step in enumerate(PAIRS[k]):
            if step != 0:
                slot = self.target.at[k, spot, p.y]
                self.arrived(slot, NEAREST.index(step), (p.along_z(step), p.slab))
                self.pass_on(k, spot, slot)

    def forward(self, k):
        p = self.p
        for spot in (0, 1):
            for way, step in ((0, 1), (1, -1)):
                order = (k * 2 + spot) * 2 + way
                slot = self.target.at[k, spot, p.row(-step)]
                self.arrived(slot, 7 + order, (p.along_y(-step), p.slab))
                half = self.target.at[k, spot, p.row(-step), way]
                self.start(half, half, 23 + order, 23 + order, (p.along_y(step), p.slab))

    def finish(self, k):
        p = self.p
        for spot in (0, 1):
            for way, step in ((0, 1), (1, -1)):
                order = (k * 2 + spot) * 2 + way
                self.arrived(
                    self.target.at[k, spot, p.row(2), way],
                    23 + order,
                    (p.along_y(-step), p.slab),
                )


class Scatter:
    COPIES = 6 * GROUPS + 7

    def __init__(self, place, terms, far, near, mixed, rows, column, sends, receives):
        self.p, self.terms = place, terms
        self.far, self.near, self.mixed, self.rows, self.column = far, near, mixed, rows, column
        self.start, self.arrived, self.drain = sender(sends, receives)

    @staticmethod
    def scratch():
        return [
            pltpu.VMEM((GROUPS, 2, BREADTH, 2, 32, N), BF16),
            pltpu.VMEM((GROUPS, 2, 2, 32, N), BF16),
            pltpu.VMEM((GROUPS, 2, 2, 2, 32, N), BF16),
            pltpu.VMEM((GROUPS, 2, 2, 32, N), BF16),
            pltpu.VMEM((GROUPS, 2, 2, 32, N), BF16),
            pltpu.VMEM((DEPTH - 1, 2, 32, N), BF16),
            pltpu.SemaphoreType.DMA((Scatter.COPIES,)),
            pltpu.SemaphoreType.DMA((Scatter.COPIES,)),
        ]

    def begin(self, k):
        p, base = self.p, 6 * k
        for way, step in ((0, 1), (1, -1)):
            self.start(
                self.terms.at[k, :, p.row(2), way],
                self.far.at[k, way],
                base + way,
                base + way,
                (p.along_y(step), p.slab),
            )
        for way, step in ((0, 1), (1, -1)):
            self.start(
                self.terms.at[k, :, p.row(step), 1 - way],
                self.near.at[k, way, 1 - way],
                base + 2 + way,
                base + 2 + way,
                (p.along_y(step), p.slab),
            )

    def forward(self, k):
        p, base = self.p, 6 * k
        for way, step in ((0, 1), (1, -1)):
            self.arrived(self.far.at[k, way], base + way, (p.along_y(-step), p.slab))
            self.mixed[k, way] = (
                self.far[k, way].astype(F32) + self.terms[k, :, p.row(step), way].astype(F32)
            ).astype(BF16)
            self.start(
                self.mixed.at[k, way],
                self.near.at[k, way, way],
                base + 4 + way,
                base + 4 + way,
                (p.along_y(step), p.slab),
            )

    def columns(self, k):
        p, base = self.p, 6 * k
        for way, step in ((0, 1), (1, -1)):
            beside = (p.along_y(-step), p.slab)
            self.arrived(self.near.at[k, way, 1 - way], base + 2 + way, beside)
            self.arrived(self.near.at[k, way, way], base + 4 + way, beside)
        for spot, step in enumerate(PAIRS[k]):
            for part in (0, 1):
                self.rows[k, spot, part] = (
                    self.terms[k, spot, p.y, part].astype(F32)
                    + self.near[k, 0, part, spot].astype(F32)
                    + self.near[k, 1, part, spot].astype(F32)
                ).astype(BF16)
            if step != 0:
                order = NEAREST.index(step)
                self.start(
                    self.rows.at[k, spot],
                    self.column.at[order],
                    6 * GROUPS + order,
                    6 * GROUPS + order,
                    (p.along_z(step), p.slab),
                )

    def total(self):
        p = self.p
        value = self.rows[0, 0].astype(F32)
        for order, step in enumerate(NEAREST):
            self.arrived(
                self.column.at[order], 6 * GROUPS + order, (p.along_z(-step), p.slab)
            )
            value = value + self.column[order].astype(F32)
        return value


class Total:
    COPIES = 17

    def __init__(self, place, held, shared, sends, receives):
        self.p, self.held, self.shared = place, held, shared
        self.start, self.arrived, self.drain = sender(sends, receives)

    @staticmethod
    def scratch(height, shared):
        return [
            pltpu.VMEM((12, height, 128), F32),
            pltpu.VMEM((8, shared, 128), F32),
            pltpu.SemaphoreType.DMA((Total.COPIES,)),
            pltpu.SemaphoreType.DMA((Total.COPIES,)),
        ]

    def along_z(self, value):
        p = self.p
        self.held[p.z] = value
        for order, step in enumerate(NEAREST):
            self.start(
                self.held.at[p.z], self.held.at[p.z], order, order, (p.along_z(step), p.slab)
            )

    def sum_z(self):
        p = self.p
        for order, step in enumerate(NEAREST):
            self.arrived(
                self.held.at[(p.z - step + DEPTH) % DEPTH], order, (p.along_z(-step), p.slab)
            )
        value = self.held[0]
        for place in range(1, DEPTH):
            value = value + self.held[place]
        return value

    def along_y(self, value):
        p = self.p
        self.held[DEPTH + p.y] = value
        for step in (1, 2, 3):
            self.start(
                self.held.at[DEPTH + p.y],
                self.held.at[DEPTH + p.y],
                6 + step,
                6 + step,
                (p.along_y(step), p.slab),
            )

    def sum_y(self):
        p = self.p
        for step in (1, 2, 3):
            self.arrived(
                self.held.at[DEPTH + p.row(-step)], 6 + step, (p.along_y(-step), p.slab)
            )
        value = self.held[DEPTH]
        for place in range(1, BREADTH):
            value = value + self.held[DEPTH + place]
        return value

    def along_slab(self, value):
        p = self.p
        self.shared[p.slab] = value
        for step in range(1, 8):
            self.start(
                self.shared.at[p.slab],
                self.shared.at[p.slab],
                9 + step,
                9 + step,
                (p.coil, (p.slab + step) % 8),
            )

    def sum_slab(self):
        p = self.p
        for step in range(1, 8):
            back = (p.slab - step + 8) % 8
            self.arrived(self.shared.at[back], 9 + step, (p.coil, back))
        value = self.shared[0]
        for place in range(1, 8):
            value = value + self.shared[place]
        return value


def region(place, body):
    def once(turn, carry):
        body()
        return carry

    lax.fori_loop(0, 1 + place.coil // 32, once, 0)


def whole(value):
    return jnp.sum(jnp.sum(value, axis=1, keepdims=True), axis=0, keepdims=True)


def front(place, k, maps, image, plane, out):
    cosine, sine = plane[0], plane[1]
    reals, imags = [], []
    for spot, step in enumerate(PAIRS[k]):
        part = pl.ds(place.first(step), BREADTH)
        maps_re, maps_im = maps[0, part, 0].astype(F32), maps[0, part, 1].astype(F32)
        image_re = image[k, spot, :, 0].astype(F32)
        image_im = image[k, spot, :, 1].astype(F32)
        reals.append((maps_re * image_re - maps_im * image_im).astype(BF16).reshape(128, N))
        imags.append((maps_re * image_im + maps_im * image_re).astype(BF16).reshape(128, N))
    real, imag = jnp.concatenate(reals, axis=0), jnp.concatenate(imags, axis=0)
    both = ((1,), (1,))
    rows_re = dot(cosine, real, both) + dot(sine, imag, both)
    rows_im = dot(cosine, imag, both) - dot(sine, real, both)
    out[k, :, 0] = rows_re.astype(BF16).reshape(8, 32, N)
    out[k, :, 1] = rows_im.astype(BF16).reshape(8, 32, N)


def readouts(place, k, blocks, plane, wide):
    cosine, sine = plane[0], plane[1]

    def lines(part):
        pieces = [blocks[k, s, part] for s in range(8)]
        return jnp.concatenate(
            [
                jnp.concatenate([piece[:, 32 * j : 32 * j + 32] for piece in pieces], axis=1)
                for j in range(8)
            ],
            axis=0,
        )

    real, imag = lines(0), lines(1)
    out_re = (dot(real, cosine) + dot(imag, sine)).reshape(2, BREADTH, 32, N)
    out_im = (dot(imag, cosine) - dot(real, sine)).reshape(2, BREADTH, 32, N)
    for spot, step in enumerate(PAIRS[k]):
        part = pl.ds(place.first(step), BREADTH)
        wide[part, 0] = out_re[spot]
        wide[part, 1] = out_im[spot]


def unread(place, k, wide, plane, out):
    cosine, sine = plane[0], plane[1]

    def lines(which):
        return jnp.concatenate(
            [
                wide[pl.ds(place.first(step), BREADTH), which].reshape(128, N).astype(BF16)
                for step in PAIRS[k]
            ],
            axis=0,
        )

    real, imag = lines(0), lines(1)
    for which, value in (
        (0, dot(real, cosine) - dot(imag, sine)),
        (1, dot(imag, cosine) + dot(real, sine)),
    ):
        value = value.astype(BF16).reshape(8, 32, N)
        for s in range(8):
            out[k, s, which] = jnp.concatenate(
                [value[j][:, 32 * s : 32 * s + 32] for j in range(8)], axis=1
            )


def unfront(place, k, blocks, maps, plane, terms):
    cosine, sine = plane[0], plane[1]
    real, imag = blocks[k, :, 0].reshape(N, N), blocks[k, :, 1].reshape(N, N)
    first = ((0,), (0,))
    image_re = dot(real, cosine, first) - dot(imag, sine, first)
    image_im = dot(imag, cosine, first) + dot(real, sine, first)
    image_re = image_re.reshape(2, BREADTH, 32, N)
    image_im = image_im.reshape(2, BREADTH, 32, N)
    for spot, step in enumerate(PAIRS[k]):
        part = pl.ds(place.first(step), BREADTH)
        maps_re, maps_im = maps[0, part, 0].astype(F32), maps[0, part, 1].astype(F32)
        terms[k, spot, :, 0] = (maps_re * image_re[spot] + maps_im * image_im[spot]).astype(BF16)
        terms[k, spot, :, 1] = (maps_re * image_im[spot] - maps_im * image_re[spot]).astype(BF16)


def strip(ref, part, at):
    return ref[:, part, at, :].reshape(N, N).astype(BF16)


def across(cosine, sine, real, imag):
    return (
        (dot(cosine, real) + dot(sine, imag)).reshape(NZ, 8, N),
        (dot(cosine, imag) - dot(sine, real)).reshape(NZ, 8, N),
    )


def fold(value):
    return jnp.sum(value[:, :, :128] + value[:, :, 128:], axis=0)


def narrow(value):
    value = value.reshape(64, N)
    value = value[:, :128] + value[:, 128:]
    return jnp.sum(value.reshape(8, 8, 128), axis=0)


def strips(body, start):
    return lax.fori_loop(
        0, 4, lambda c, carry: body(pl.ds(pl.multiple_of(c * 8, 8), 8), carry), start
    )


def filtered(wide, weight, depth, kept):
    cosine, sine = depth[0], depth[1]

    def chunk(at, total):
        real, imag = across(cosine, sine, strip(wide, 0, at), strip(wide, 1, at))
        kept[:, 0, at, :] = real
        kept[:, 1, at, :] = imag
        scale = weight[:, at, :]
        real, imag = scale * real, scale * imag
        total = total + fold(real * real + imag * imag)
        real = (scale * real).astype(BF16).reshape(N, N)
        imag = (scale * imag).astype(BF16).reshape(N, N)
        wide[:, 0, at, :] = (dot(cosine, real) - dot(sine, imag)).reshape(NZ, 8, N)
        wide[:, 1, at, :] = (dot(cosine, imag) + dot(sine, real)).reshape(NZ, 8, N)
        return total

    return strips(chunk, jnp.zeros((8, 128), F32))


def closing(wide, wide_saved, first, weight, data, depth, kept):
    cosine, sine = depth[0], depth[1]

    def chunk(at, totals):
        real, imag = across(cosine, sine, strip(wide, 0, at), strip(wide, 1, at))
        kept[:, 0, at, :] = real
        kept[:, 1, at, :] = imag
        saved_re, saved_im = across(
            cosine, sine, strip(wide_saved, 0, at), strip(wide_saved, 1, at)
        )
        first_re, first_im = first[:, 0, at, :], first[:, 1, at, :]
        scale = weight[:, at, :]
        square = scale * scale
        second, mixed = totals
        second = second + fold(square * (real * real + imag * imag))
        mixed = mixed + fold(square * (real * first_re + imag * first_im))
        target_re = data[0, :, 0, at, :].astype(F32) - 2.0 * scale * saved_re
        target_im = data[0, :, 1, at, :].astype(F32) - 2.0 * scale * saved_im
        sampled = jnp.where(scale != 0.0, 1.0, 0.0)
        wide[:, 0, at, :] = sampled * (first_re * target_re + first_im * target_im)
        wide[:, 1, at, :] = sampled * (real * target_re + imag * target_im)
        return second, mixed

    zero = jnp.zeros((8, 128), F32)
    return strips(chunk, (zero, zero))


COUNTS = (4, 4, 4, 5, 5, 5, 5, 8, 4, 4)


def scratch_shapes():
    return (
        Gather.scratch() * 3
        + Exchange.scratch() * 4
        + Scatter.scratch()
        + Total.scratch(16, 16)
        + Total.scratch(40, 8)
        + [pltpu.VMEM((NZ, 2, 32, N), F32)] * 4
    )


def kernel(
    cotangent, saved, maps, data, weight, gain, plane, depth, image_grad, kspace_grad, logit_grad, *scratch
):
    parts, at = [], 0
    for count in COUNTS:
        parts.append(scratch[at : at + count])
        at += count
    wide, wide_saved, first, second = scratch[at:]
    place = Place()
    gather = Gather(place, *parts[0])
    gather_saved = Gather(place, *parts[1])
    gather_next = Gather(place, *parts[2])
    ahead = Exchange(place, *parts[3])
    ahead_saved = Exchange(place, *parts[4])
    back = Exchange(place, *parts[5])
    ahead_next = Exchange(place, *parts[6])
    scatter = Scatter(place, *parts[7])
    early_sums = Total(place, *parts[8])
    late_sums = Total(place, *parts[9])

    direction = cotangent[0]
    gather.source[...] = direction.astype(BF16)
    gather_saved.source[...] = saved[0].astype(BF16)
    norm_part = narrow(direction * direction)
    greet(place)

    def turn_out(g, e, k):
        g.finish(k)
        region(place, lambda: front(place, k, maps, g.target, plane, e.source))
        e.begin(k)

    def arrive(e, k, to):
        e.finish(k)
        region(place, lambda: readouts(place, k, e.target, plane, to))

    gather.begin()
    gather.spread(0)
    gather.spread(1)
    gather.forward(0)
    gather.spread(2)
    gather.forward(1)
    turn_out(gather, ahead, 0)
    gather.spread(3)
    gather.forward(2)
    turn_out(gather, ahead, 1)
    ahead.forward(0)
    gather.forward(3)
    turn_out(gather, ahead, 2)
    ahead.forward(1)
    turn_out(gather, ahead, 3)
    gather_saved.begin()
    ahead.forward(2)
    arrive(ahead, 0, wide)
    ahead.forward(3)
    arrive(ahead, 1, wide)
    arrive(ahead, 2, wide)
    arrive(ahead, 3, wide)
    gather_saved.spread(0)
    gather_saved.spread(1)
    gather_saved.spread(2)
    gather_saved.spread(3)
    energy = filtered(wide, weight, depth, first)

    early_sums.along_z(jnp.concatenate([norm_part, energy], axis=0))
    for k in range(GROUPS):
        region(place, lambda: unread(place, k, wide, plane, back.source))
        back.begin(k)
        gather_saved.forward(k)
    early_sums.along_y(early_sums.sum_z())
    back.forward(0)
    gather_saved.finish(0)
    region(
        place, lambda: front(place, 0, maps, gather_saved.target, plane, ahead_saved.source)
    )
    back.forward(1)
    for k in range(GROUPS):
        back.finish(k)
        region(place, lambda: unfront(place, k, back.target, maps, plane, scatter.terms))
        scatter.begin(k)
        if k + 2 < GROUPS:
            back.forward(k + 2)
        if k >= 1:
            scatter.forward(k - 1)
        if k >= 2:
            scatter.columns(k - 2)
        if k == 1:
            early_sums.along_slab(early_sums.sum_y())
    ahead_saved.begin(0)
    scatter.forward(3)
    scatter.columns(2)
    turn_out(gather_saved, ahead_saved, 1)
    scatter.columns(3)
    turn_out(gather_saved, ahead_saved, 2)
    turn_out(gather_saved, ahead_saved, 3)
    sums = early_sums.sum_slab()
    norm, first_energy = whole(sums[0:8]), whole(sums[8:16])
    alpha = norm / (first_energy + DAMPING * norm)
    direction = cotangent[0]
    residual = direction - alpha[None] * (scatter.total() + DAMPING * direction)
    gather_next.source[...] = residual.astype(BF16)
    image_grad[0] = residual

    gather_next.begin()
    for k in range(GROUPS):
        ahead_saved.forward(k)
    gather_next.spread(0)
    gather_next.spread(1)
    gather_next.forward(0)
    gather_next.spread(2)
    gather_next.forward(1)
    turn_out(gather_next, ahead_next, 0)
    gather_next.spread(3)
    gather_next.forward(2)
    turn_out(gather_next, ahead_next, 1)
    ahead_next.forward(0)
    gather_next.forward(3)
    turn_out(gather_next, ahead_next, 2)
    ahead_next.forward(1)
    turn_out(gather_next, ahead_next, 3)
    arrive(ahead_saved, 0, wide_saved)
    ahead_next.forward(2)
    arrive(ahead_saved, 1, wide_saved)
    ahead_next.forward(3)
    arrive(ahead_saved, 2, wide_saved)
    arrive(ahead_saved, 3, wide_saved)
    for k in range(GROUPS):
        arrive(ahead_next, k, wide)
    second_energy, mixed_energy = closing(wide, wide_saved, first, weight, data, depth, second)

    residual = image_grad[0]
    late_sums.along_z(
        jnp.concatenate(
            [
                jnp.concatenate(
                    [
                        jnp.sum(wide[:, 0], axis=2),
                        jnp.sum(wide[:, 1], axis=2),
                        jnp.zeros((NZ, 64), F32),
                    ],
                    axis=1,
                ),
                jnp.sum(second_energy, axis=0, keepdims=True),
                jnp.sum(mixed_energy, axis=0, keepdims=True),
                jnp.sum(narrow(residual * residual), axis=0, keepdims=True),
                jnp.sum(narrow(residual * direction), axis=0, keepdims=True),
                jnp.zeros((4, 128), F32),
            ],
            axis=0,
        )
    )
    late_sums.along_y(late_sums.sum_z())
    lines = late_sums.sum_y()
    late_sums.along_slab(lines[32:40])
    scalars = jnp.sum(late_sums.sum_slab(), axis=1, keepdims=True)
    second_all, mixed_all, norm_next, crossing = [scalars[k : k + 1] for k in range(4)]
    beta = norm_next / norm
    curvature = (second_all + beta * (2.0 * mixed_all + beta * first_energy)) + DAMPING * (
        norm_next + beta * (2.0 * crossing + beta * norm)
    )
    later = norm_next / curvature
    earlier = alpha + later * beta
    image_grad[0] = DAMPING * (earlier[None] * direction + later[None] * residual)
    logit_grad[...] = gain[...] * (earlier * lines[0:32, 0:32] + later * lines[0:32, 32:64])

    def write(at, carry):
        scale = weight[:, at, :]
        for part in (0, 1):
            kept = earlier[None] * first[:, part, at, :] + later[None] * second[:, part, at, :]
            wide[:, part, at, :] = scale * kept
        return carry

    strips(write, 0)
    kspace_grad[0] = wide[...].astype(BF16)
    for part in (
        gather, gather_saved, gather_next, ahead, ahead_saved, back, ahead_next, scatter, early_sums, late_sums
    ):
        part.drain()


def shards(cotangent, saved_solution, coil_maps, kspace, mask_logit, reach):
    plane, depth = tables()
    centred = (jnp.arange(N, dtype=jnp.int32) + N // 2) % N
    sampled = (centred[None, None, :] >= (N - reach)[:, :, None]).astype(F32)
    gate = jax.nn.sigmoid(mask_logit)
    weight = sampled * gate[:, :, None]
    whole_vmem = pl.BlockSpec(memory_space=pltpu.VMEM)
    image_grad, kspace_grad, logit_grad = pl.pallas_call(
        kernel,
        out_shape=(
            jax.ShapeDtypeStruct((1, 2, 32, N), F32),
            jax.ShapeDtypeStruct((1, NZ, 2, 32, N), BF16),
            jax.ShapeDtypeStruct((NZ, 32), F32),
        ),
        in_specs=[whole_vmem] * 8,
        out_specs=[whole_vmem] * 3,
        scratch_shapes=scratch_shapes(),
        compiler_params=pltpu.CompilerParams(
            collective_id=0, has_side_effects=True, vmem_limit_bytes=60 * 1024 * 1024
        ),
        name="pass",
    )(cotangent, saved_solution, coil_maps, kspace, weight, gate * (1.0 - gate), plane, depth)
    return (image_grad, kspace_grad, logit_grad)


def solution(mesh):
    placed = (
        P("coil", None, "slab", None),
        P("coil", None, "slab", None),
        P("coil", None, None, "slab", None),
        P("coil", None, None, "slab", None),
        P(None, "slab"),
        P(None, "slab"),
    )
    return jax.shard_map(
        shards,
        mesh=mesh,
        in_specs=placed,
        out_specs=(
            P("coil", None, "slab", None),
            P("coil", None, None, "slab", None),
            P(None, "slab"),
        ),
        check_vma=False,
    )
```
